32 devices in a mesh: dp: 8 (over z, x), rep: 4 (over y, core).
Axes of the slice: x: 2, y: 2, z: 4, core: 2. Of those that a mesh axis runs over, the one named last changes fastest.
Arguments:
- tokens: bfloat16 [32, 512, 1024], P(('dp', 'rep')), may hold values from -6 to 6
- segment_ids: int32 [32, 512], P(('dp', 'rep')), may hold values from 0 to 3, never falling along the last dimension, each value on 1 to 256 neighbouring positions
- cotangent: bfloat16 [32, 512, 1024], P(('dp', 'rep')), may hold values from -6 to 6
- norm_in_gain: bfloat16 [1024], P('dp'), may hold values from 0.5 to 1.5
- norm_in_shift: bfloat16 [1024], P('dp'), may hold values from -3 to 3
- qkv_weight: bfloat16 [1024, 3072], P('dp'), may hold values from -0.1875 to 0.1875
- qkv_bias: bfloat16 [3072], P('dp'), may hold values from -3 to 3
- proj_weight: bfloat16 [1024, 1024], P('dp'), may hold values from -1 to 1
- proj_bias: bfloat16 [1024], P('dp'), may hold values from -3 to 3
- norm_mid_gain: bfloat16 [1024], P('dp'), may hold values from 0.5 to 1.5
- norm_mid_shift: bfloat16 [1024], P('dp'), may hold values from -3 to 3
- up_weight: bfloat16 [1024, 4096], P('dp'), may hold values from -0.1875 to 0.1875
- up_bias: bfloat16 [4096], P('dp'), may hold values from -3 to 3
- down_weight: bfloat16 [4096, 1024], P('dp'), may hold values from -0.09375 to 0.09375
- down_bias: bfloat16 [1024], P('dp'), may hold values from -3 to 3
- prefix_table: bfloat16 [10, 1024], replicated, may hold values from -6 to 6
- first_weight: bfloat16 [1024, 800], P(None, 'rep'), may hold values from -0.1875 to 0.1875
- first_bias: bfloat16 [800], P('rep'), may hold values from -3 to 3
- second_weight: bfloat16 [800, 2048], P('rep', 'dp'), may hold values from -0.3125 to 0.3125
- second_bias: bfloat16 [2048], P('dp'), may hold values from -3 to 3
Outputs:
- activations: bfloat16 [32, 512, 1024], P(('dp', 'rep'))
- input_grad: float32 [32, 512, 1024], P(('dp', 'rep'))
- prefix_table_grad: float32 [10, 1024], replicated
- first_weight_grad: float32 [1024, 800], P(None, 'rep')
- first_bias_grad: float32 [800], P('rep')
- second_weight_grad: float32 [800, 2048], P('rep', 'dp')
- second_bias_grad: float32 [2048], P('dp')
- prefix_kv: float32 [10, 2048], replicated
The draws below stay inside these ranges and needn't reach their ends.
Inputs may be any that keep to these rules, and one draw needn't show every extreme that they name: `segment_ids`: within each packed row of 512 tokens the ids never fall; each id names one run of consecutive tokens, of 1 to 256 tokens, and some run has exactly that many.
All inputs are finite; a program needn't handle non-finite values.
Results may differ from the reference program's by a relative error of at most 0.01.
The reference program's roundings to bfloat16 on the way count: a program that leaves them out, or rounds other values in their place, can miss the bound.
Values may be sent and summed in bfloat16 or wider, within the bound.
A program may use at most 192 MiB of HBM per device.

```python
import math
import jax
import jax.numpy as jnp
import numpy as np
from jax import lax

D = 1024
HEADS = 16
HEAD_DIM = 64
FF = 4096
PREFIX = 10
R = 800
TOK_DEV = 512
SEGS = 4
NROWS = 32
KV = 2048


def block_scale(key, shape, cuts, least, largest):
    def one(position, blocks):
        heights = jax.random.uniform(jax.random.fold_in(jax.random.fold_in(key, 6), position), (blocks,), jnp.float32, least / len(cuts), largest / len(cuts))
        return jnp.repeat(jnp.exp(heights), shape[position] // blocks).reshape((-1,) + (1,) * (len(shape) - position - 1))

    level = one(*cuts[0])
    for cut in cuts[1:]:
        level = level * one(*cut)
    return level


def length_profile(number_of, total, bound, skew):
    portions = [(1 << 20) // math.isqrt(standing ** skew) + 1 for standing in range(2, number_of + 1)]
    spare, counts = total - bound - (number_of - 1), [1] * (number_of - 1)
    while spare > 0:
        candidates = [i for i in range(number_of - 1) if counts[i] < bound]
        mass, left = sum([portions[i] for i in candidates]), spare
        for i in candidates:
            extra = min(bound - counts[i], max(1, left * portions[i] // mass), spare)
            counts[i] = counts[i] + extra
            spare = spare - extra
    return np.array([bound] + counts)


def ragged(rng, amount, total, reach, skew):
    if amount == 2:
        one = jax.random.randint(rng, (), max(1, total - reach), min(reach, total - 1) + 1)
        return jnp.stack([one, total - one])
    lengths = jnp.asarray(length_profile(amount, total, reach, skew), jnp.int32)
    pairs = (amount - 1) // 2
    giver, sink = lengths[1:1 + 2 * pairs:2], lengths[2:2 + 2 * pairs:2]
    slack = jnp.minimum(giver - 1, reach - sink)
    moved = jax.random.randint(jax.random.fold_in(rng, 1), (pairs,), 0, 1 << 20) % (slack + 1)
    lengths = lengths.at[1:1 + 2 * pairs:2].set(giver - moved).at[2:2 + 2 * pairs:2].set(sink + moved)
    return lengths[jax.random.permutation(jax.random.fold_in(rng, 2), amount)]


def scatter_about(key, shape, width, most, pieces=(), kind=jnp.bfloat16):
    array = width * jax.random.normal(key, shape, jnp.float32)
    if pieces:
        array = array * block_scale(key, shape, pieces, -0.22, 0.18)
    return jnp.clip(array, -most, most).astype(kind)


def setup_inputs(seed: int = 0) -> dict:
    arg_keys = jax.random.split(jax.random.key(seed), 21)
    return {
        "tokens": scatter_about(arg_keys[0], (NROWS, TOK_DEV, D), 1.0, 6.0, ((0, 32),)),
        "segment_ids": jax.vmap(lambda own: jnp.searchsorted(jnp.cumsum(ragged(own, SEGS, TOK_DEV, TOK_DEV // 2, 0)), jnp.arange(TOK_DEV), side="right"))(jax.random.split(arg_keys[1], NROWS)).reshape((NROWS, TOK_DEV)).astype(jnp.int32),
        "cotangent": scatter_about(arg_keys[2], (NROWS, TOK_DEV, D), 1.0, 6.0, ((0, 32),)),
        "norm_in_gain": jnp.clip(1.0 + 0.1 * jax.random.normal(arg_keys[3], (D,), jnp.float32), 0.5, 1.5).astype(jnp.bfloat16),
        "norm_in_shift": scatter_about(arg_keys[4], (D,), 0.5, 3.0, ((0, 8),)),
        "qkv_weight": scatter_about(arg_keys[5], (D, 3 * D), D ** -0.5, 0.1875, ((0, 8),)),
        "qkv_bias": scatter_about(arg_keys[6], (3 * D,), 0.5, 3.0, ((0, 8),)),
        "proj_weight": scatter_about(arg_keys[7], (D, D), (D // 32) ** -0.5, 1.0, ((0, 8),)),
        "proj_bias": scatter_about(arg_keys[8], (D,), 0.5, 3.0, ((0, 8),)),
        "norm_mid_gain": jnp.clip(1.0 + 0.1 * jax.random.normal(arg_keys[9], (D,), jnp.float32), 0.5, 1.5).astype(jnp.bfloat16),
        "norm_mid_shift": scatter_about(arg_keys[10], (D,), 0.5, 3.0, ((0, 8),)),
        "up_weight": scatter_about(arg_keys[11], (D, FF), D ** -0.5, 0.1875, ((0, 8),)),
        "up_bias": scatter_about(arg_keys[12], (FF,), 0.5, 3.0, ((0, 8),)),
        "down_weight": scatter_about(arg_keys[13], (FF, D), FF ** -0.5, 0.09375, ((0, 8),)),
        "down_bias": scatter_about(arg_keys[14], (D,), 0.5, 3.0, ((0, 8),)),
        "prefix_table": scatter_about(arg_keys[15], (PREFIX, D), 1.0, 6.0),
        "first_weight": scatter_about(arg_keys[16], (D, R), D ** -0.5, 0.1875, ((1, 4),)),
        "first_bias": scatter_about(arg_keys[17], (R,), 0.5, 3.0, ((0, 4),)),
        "second_weight": scatter_about(arg_keys[18], (R, KV), (R // 2) ** -0.5, 0.3125, ((0, 4), (1, 8))),
        "second_bias": scatter_about(arg_keys[19], (KV,), 0.5, 3.0, ((0, 8),)),
    }


@jax.custom_vjp
def low(v):
    return lax.optimization_barrier(v.astype(jnp.bfloat16)).astype(jnp.float32)

@jax.custom_vjp
def low_back(v):
    return v

def low_keep(v):
    return (low(v), None)

def low_pass(kept, grad):
    return (grad,)

def back_keep(v):
    return (v, None)

def back_low(kept, grad):
    return (low(grad),)
low.defvjp(low_keep, low_pass)
low_back.defvjp(back_keep, back_low)
eps_norm = 1e-05
neg_fill = -1e+30
highest = lax.Precision.HIGHEST

def matmul(left, right):
    return jnp.dot(left, right, precision=highest, preferred_element_type=jnp.float32)

def layer_norm(values, gain, shift):
    centred = values - lax.optimization_barrier(jnp.mean(values, axis=-1, keepdims=True))
    variance = lax.optimization_barrier(jnp.mean(centred * centred, axis=-1, keepdims=True))
    return centred * lax.rsqrt(variance + eps_norm) * gain + shift

def row_forward(row_tokens, row_segments, prefix_low, frozen):
    gain_in, shift_in, qkv_full, qkv_shift, proj_full, proj_shift, gain_mid, shift_mid, up_full, up_shift, down_full, down_shift = frozen
    length = row_tokens.shape[0]
    normed_in = low(layer_norm(row_tokens, gain_in, shift_in))
    packed = low_back(low(matmul(normed_in, qkv_full) + qkv_shift))
    queries = packed[:, :D].reshape(length, HEADS, HEAD_DIM)
    key_all = jnp.concatenate([prefix_low[:, :D], packed[:, D:2 * D]], axis=0).reshape(-1, HEADS, HEAD_DIM)
    value_all = jnp.concatenate([prefix_low[:, D:], packed[:, 2 * D:]], axis=0).reshape(-1, HEADS, HEAD_DIM)
    raw_scores = jnp.einsum('qhd,khd->hqk', queries, key_all, precision=highest)
    scores = low_back(raw_scores * HEAD_DIM ** (-0.5))
    positions = jnp.arange(length)
    own_keys = (row_segments[:, None] == row_segments[None, :]) & (positions[None, :] <= positions[:, None])
    allowed = jnp.concatenate([jnp.ones((length, PREFIX), dtype=bool), own_keys], axis=1)
    scores = jnp.where(allowed[None], scores, neg_fill)
    soft_probs = jax.nn.softmax(scores, axis=-1)
    attended = jnp.einsum('hqk,khd->qhd', low(soft_probs), value_all, precision=highest).reshape(length, D)
    attended = low_back(low(attended))
    residual = row_tokens + low_back(matmul(attended, proj_full) + proj_shift)
    normed_mid = low(layer_norm(residual, gain_mid, shift_mid))
    pre_act = low_back(matmul(normed_mid, up_full) + up_shift)
    activated = low(jax.nn.gelu(pre_act, approximate=True))
    return residual + low_back(matmul(activated, down_full) + down_shift)

def reference(tokens, segment_ids, cotangent, norm_in_gain, norm_in_shift, qkv_weight, qkv_bias, proj_weight, proj_bias, norm_mid_gain, norm_mid_shift, up_weight, up_bias, down_weight, down_bias, prefix_table, first_weight, first_bias, second_weight, second_bias):
    frozen = tuple((member.astype(jnp.float32) for member in (norm_in_gain, norm_in_shift, qkv_weight, qkv_bias, proj_weight, proj_bias, norm_mid_gain, norm_mid_shift, up_weight, up_bias, down_weight, down_bias)))
    rows_total = tokens.shape[0]
    group_rows = math.gcd(rows_total, max(1, 4096 // TOK_DEV))
    group_count = rows_total // group_rows

    def forward(token_rows, table, first_full, first_shift, second_full, second_shift):
        hidden = low(jnp.tanh(matmul(table, first_full) + first_shift))
        prefix_kv = matmul(hidden, second_full) + second_shift
        prefix_low = low(prefix_kv)

        def one_group(group_pair):
            group_tokens, group_segments = group_pair

            def one_row(row_tokens, row_segments):
                return row_forward(row_tokens, row_segments, prefix_low, frozen)
            return jax.vmap(one_row)(group_tokens, group_segments)
        outputs = lax.map(jax.checkpoint(one_group), (token_rows.reshape(group_count, group_rows, TOK_DEV, D), segment_ids.reshape(group_count, group_rows, TOK_DEV)))
        return (outputs.reshape(rows_total, TOK_DEV, D), prefix_kv)
    outputs, pullback, prefix_kv = jax.vjp(forward, tokens.astype(jnp.float32), prefix_table.astype(jnp.float32), first_weight.astype(jnp.float32), first_bias.astype(jnp.float32), second_weight.astype(jnp.float32), second_bias.astype(jnp.float32), has_aux=True)
    grads = pullback(cotangent.astype(jnp.float32))
    return (outputs.astype(jnp.bfloat16), grads[0], grads[1], grads[2], grads[3], grads[4], grads[5], prefix_kv)
```

```python
import functools

import jax
import jax.numpy as jnp
from jax import lax
from jax.experimental import pallas as pl
from jax.experimental.pallas import tpu as pltpu
from jax.sharding import PartitionSpec as P

HEAD_DIM = 64
PAIR = 2 * HEAD_DIM
SLOT = 512
PAD = 16

eps_norm = 1e-05
neg_fill = -1e30
highest = lax.Precision.HIGHEST
f32 = jnp.float32
bf16 = jnp.bfloat16

NN = (((1,), (0,)), ((), ()))
NT = (((1,), (1,)), ((), ()))
TN = (((0,), (0,)), ((), ()))


def mm(left, right, dims=NN):
    return lax.dot_general(left, right, dims, preferred_element_type=f32)


def normalise(values):
    centred = values - jnp.mean(values, axis=-1, keepdims=True)
    variance = jnp.mean(centred * centred, axis=-1, keepdims=True)
    inverse = lax.rsqrt(variance + eps_norm)
    return centred * inverse, inverse


def norm_backward(values, gain, upstream):
    unit, inverse = normalise(values)
    scaled = upstream * gain
    return inverse * (
        scaled
        - jnp.mean(scaled, axis=-1, keepdims=True)
        - unit * jnp.mean(scaled * unit, axis=-1, keepdims=True)
    )


def block_kernel(
    shards,
    prefix_count,
    tokens_hbm,
    cotangent_hbm,
    seg_col,
    seg_row,
    vec_ref,
    prefix_ref,
    weights_hbm,
    activations_hbm,
    input_grad_hbm,
    prefix_grad_ref,
    weights,
    tok,
    cot,
    normed,
    packed,
    keys_t,
    values_t,
    probs,
    bias_t,
    key_pre,
    value_pre,
    pre_f32,
    pre_probs,
    pre_dscore,
    mixed_t,
    acc_a,
    acc_g,
    resid,
    attended,
    grad_packed,
    sem,
    wsem,
):
    length, width = tok.shape
    heads = width // HEAD_DIM
    unit = width // shards
    half = width // SLOT
    scale = HEAD_DIM ** (-0.5)
    group = shards // half

    copies = [
        pltpu.make_async_copy(tokens_hbm, tok, sem.at[0]),
        pltpu.make_async_copy(cotangent_hbm, cot, sem.at[1]),
    ]
    for c in copies:
        c.start()
    blocks = 12
    loads = [
        pltpu.make_async_copy(
            weights_hbm.at[:, pl.ds(b * unit, unit), :],
            weights.at[:, pl.ds(b * unit, unit), :],
            wsem.at[b],
        )
        for b in range(blocks)
    ]
    for c in loads:
        c.start()

    def in_weight(block, col):
        return weights[:, pl.ds(block * unit, unit), pl.ds(col, SLOT)].reshape(width, SLOT)

    def out_weight(block, c):
        return weights[pl.ds(c * group, group), pl.ds(block * unit, unit), :].reshape(SLOT, width)

    def vec(row, col=0, size=None):
        return vec_ref[pl.ds(row, 1), pl.ds(col, width if size is None else size)]

    rows_step = 128
    row_steps = length // rows_step

    copies[0].wait()

    @pl.loop(0, row_steps)
    def _(r):
        rows = pl.ds(r * rows_step, rows_step)
        unit_rows, _ = normalise(tok[rows, :].astype(f32))
        normed[rows, :] = (unit_rows * vec(0) + vec(1)).astype(bf16)
        key_pos = lax.broadcasted_iota(jnp.int32, (rows_step, length), 0) + r * rows_step
        query_pos = lax.broadcasted_iota(jnp.int32, (rows_step, length), 1)
        allowed = (seg_col[rows, :] == seg_row[...]) & (key_pos <= query_pos)
        bias_t[rows, :] = jnp.where(allowed, 0.0, neg_fill)

    head_of_row = lax.broadcasted_iota(jnp.int32, (heads * PAD, width), 0) // PAD
    head_of_col = lax.broadcasted_iota(jnp.int32, (heads * PAD, width), 1) // HEAD_DIM
    own_head = head_of_row == head_of_col
    zero = jnp.zeros((), bf16)
    key_pre[...] = jnp.where(
        own_head, jnp.concatenate([prefix_ref[:, :width]] * heads, axis=0), zero
    )
    value_pre[...] = jnp.where(
        own_head, jnp.concatenate([prefix_ref[:, width:]] * heads, axis=0), zero
    )

    for b in range(3):
        loads[b].wait()

    @pl.loop(0, 3 * half)
    def _(s):
        block = s // half
        col = (s % half) * SLOT
        out = mm(normed[...], in_weight(block, col)) + vec(2 + block, col, SLOT)
        factor = jnp.where(block == 0, scale, 1.0).astype(bf16)
        packed[:, pl.ds(s * SLOT, SLOT)] = out.astype(bf16) * factor

    queries = slice(0, width)
    pre_scores = mm(key_pre[...], packed[:, queries], NT)
    pad_row = lax.broadcasted_iota(jnp.int32, pre_scores.shape, 0) % PAD
    pre_f32[...] = jnp.where(pad_row < prefix_count, pre_scores, neg_fill)

    q_blocks = ((0, length // 2, length // 2), (length // 2, length // 2, length))
    lane_head = lax.broadcasted_iota(jnp.int32, (length, PAIR), 1) // HEAD_DIM

    @pl.loop(0, heads // 2)
    def _(p):
        col = pl.multiple_of(p * PAIR, PAIR)
        q_pair = packed[:, pl.ds(col, PAIR)]
        k_pair = packed[:, pl.ds(width + col, PAIR)]
        v_pair = packed[:, pl.ds(2 * width + col, PAIR)]
        keys_t[pl.ds(col, PAIR), :] = k_pair.T
        values_t[pl.ds(col, PAIR), :] = v_pair.T
        for e in range(2):
            k_head = jnp.where(lane_head == e, k_pair, zero)
            head = 2 * p + e
            feat = pl.ds(pl.multiple_of(head * HEAD_DIM, HEAD_DIM), HEAD_DIM)
            pre_rows = pl.ds(pl.multiple_of(head * PAD, PAD), PAD)
            for q0, q_size, k_size in q_blocks:
                s = mm(k_head[:k_size], q_pair[q0 : q0 + q_size], NT)
                s = s + bias_t[:k_size, q0 : q0 + q_size]
                sp = pre_f32[pre_rows, q0 : q0 + q_size]
                top = jnp.maximum(
                    jnp.max(s, axis=0, keepdims=True), jnp.max(sp, axis=0, keepdims=True)
                )
                s = jnp.exp(s - top)
                sp = jnp.exp(sp - top)
                inverse = 1.0 / (
                    jnp.sum(s, axis=0, keepdims=True) + jnp.sum(sp, axis=0, keepdims=True)
                )
                own = (s * inverse).astype(bf16)
                probs[head, :k_size, q0 : q0 + q_size] = own
                pre_probs[pre_rows, q0 : q0 + q_size] = (sp * inverse).astype(bf16)
                mixed_t[feat, q0 : q0 + q_size] = mm(values_t[feat, :k_size], own)

    @pl.loop(0, width // 128)
    def _(i):
        rows = pl.ds(pl.multiple_of(i * 128, 128), 128)
        full = mixed_t[rows, :] + mm(value_pre[:, rows], pre_probs[...], TN)
        attended[:, rows] = full.T.astype(bf16)

    loads[3].wait()

    @pl.loop(0, half)
    def _(c):
        cols = pl.ds(pl.multiple_of(c * SLOT, SLOT), SLOT)
        out = mm(attended[...], in_weight(3, c * SLOT)) + vec(5, c * SLOT, SLOT)
        resid[:, cols] = tok[:, cols].astype(f32) + out

    @pl.loop(0, row_steps)
    def _(r):
        rows = pl.ds(r * rows_step, rows_step)
        unit_rows, _ = normalise(resid[rows, :])
        normed[rows, :] = (unit_rows * vec(6) + vec(7)).astype(bf16)

    for b in range(4, 12):
        loads[b].wait()
    copies[1].wait()

    ff_steps = 4 * half
    root = 0.7978845608028654
    cube = 0.044715

    @pl.loop(0, ff_steps)
    def _(i):
        col = (i % half) * SLOT
        w_up = in_weight(4 + i // half, col)
        w_down = weights[
            pl.ds(i * (shards // ff_steps), shards // ff_steps), pl.ds(8 * unit, 4 * unit), :
        ].reshape(SLOT, width)
        pre = mm(normed[...], w_up) + vec(8 + i // half, col, SLOT)
        square = pre * pre
        t = jnp.tanh(root * (pre + cube * (square * pre)))
        act = (0.5 * pre * (1.0 + t)).astype(bf16)
        slope = 0.5 * (1.0 + t) + (0.5 * root) * pre * (1.0 - t * t) * (
            1.0 + (3.0 * cube) * square
        )
        grad_act = mm(cot[...], w_down, NT)
        grad_pre = (grad_act * slope).astype(bf16)
        out = mm(act, w_down)
        mid = mm(grad_pre, w_up, NT)

        @pl.when(i == 0)
        def _():
            acc_a[...] = out
            acc_g[...] = mid

        @pl.when(i > 0)
        def _():
            acc_a[...] += out
            acc_g[...] += mid

    @pl.loop(0, row_steps)
    def _(r):
        rows = pl.ds(r * rows_step, rows_step)
        attended[rows, :] = (resid[rows, :] + acc_a[rows, :] + vec(12)).astype(bf16)
        grad = cot[rows, :].astype(f32) + norm_backward(resid[rows, :], vec(6), acc_g[rows, :])
        acc_g[rows, :] = grad
        normed[rows, :] = grad.astype(bf16)

    out_copy = pltpu.make_async_copy(attended, activations_hbm, sem.at[2])
    out_copy.start()
    for c in range(half):
        cot[:, c * SLOT : (c + 1) * SLOT] = mm(normed[...], out_weight(3, c), NT).astype(bf16)
    pre_f32[...] = mm(value_pre[...], cot[...], NT)

    @pl.loop(0, heads // 2)
    def _(p):
        col = pl.multiple_of(p * PAIR, PAIR)
        q_pair = packed[:, pl.ds(col, PAIR)]
        v_pair = packed[:, pl.ds(2 * width + col, PAIR)]
        g_pair = cot[:, pl.ds(col, PAIR)]
        key_grad = jnp.zeros((length, PAIR), f32)
        value_grad = jnp.zeros((length, PAIR), f32)
        for e in range(2):
            own_lanes = lane_head == e
            v_head = jnp.where(own_lanes, v_pair, zero)
            q_head = jnp.where(own_lanes, q_pair, zero)
            g_head = jnp.where(own_lanes, g_pair, zero)
            head = 2 * p + e
            feat = pl.ds(pl.multiple_of(head * HEAD_DIM, HEAD_DIM), HEAD_DIM)
            pre_rows = pl.ds(pl.multiple_of(head * PAD, PAD), PAD)
            for q0, q_size, k_size in q_blocks:
                dp = mm(v_head[:k_size], g_pair[q0 : q0 + q_size], NT)
                own_low = probs[head, :k_size, q0 : q0 + q_size]
                own = own_low.astype(f32)
                pre = pre_probs[pre_rows, q0 : q0 + q_size].astype(f32)
                pre_dp = pre_f32[pre_rows, q0 : q0 + q_size]
                dot = jnp.sum(own * dp, axis=0, keepdims=True) + jnp.sum(
                    pre * pre_dp, axis=0, keepdims=True
                )
                ds = (own * (dp - dot)).astype(bf16)
                pre_dscore[pre_rows, q0 : q0 + q_size] = (pre * (pre_dp - dot)).astype(bf16)
                mixed_t[feat, q0 : q0 + q_size] = mm(keys_t[feat, :k_size], ds)
                dk = mm(ds, q_head[q0 : q0 + q_size])
                dv = mm(own_low, g_head[q0 : q0 + q_size])
                if k_size < length:
                    fill = jnp.zeros((length - k_size, PAIR), f32)
                    dk = jnp.concatenate([dk, fill], axis=0)
                    dv = jnp.concatenate([dv, fill], axis=0)
                key_grad = key_grad + dk
                value_grad = value_grad + dv
        grad_packed[:, pl.ds(width + col, PAIR)] = key_grad.astype(bf16)
        grad_packed[:, pl.ds(2 * width + col, PAIR)] = value_grad.astype(bf16)

    @pl.loop(0, width // 128)
    def _(i):
        rows = pl.ds(pl.multiple_of(i * 128, 128), 128)
        full = mixed_t[rows, :] + mm(key_pre[:, rows], pre_dscore[...], TN)
        grad_packed[:, rows] = (full * scale).T.astype(bf16)

    for part, (left, right) in enumerate(((pre_dscore, packed), (pre_probs, cot))):
        whole = jnp.where(own_head, mm(left[...], right[:, :width]), 0.0)
        total = whole[:PAD]
        for h in range(1, heads):
            total = total + whole[h * PAD : (h + 1) * PAD]
        prefix_grad_ref[:, part * width : (part + 1) * width] = total

    for c in range(half):
        total = None
        for b in range(3):
            term = mm(grad_packed[:, b * width : (b + 1) * width], out_weight(b, c), NT)
            total = term if total is None else total + term
        acc_a[:, c * SLOT : (c + 1) * SLOT] = total

    @pl.loop(0, row_steps)
    def _(r):
        rows = pl.ds(r * rows_step, rows_step)
        acc_g[rows, :] += norm_backward(tok[rows, :].astype(f32), vec(0), acc_a[rows, :])

    in_copy = pltpu.make_async_copy(acc_g, input_grad_hbm, sem.at[3])
    in_copy.start()
    out_copy.wait()
    in_copy.wait()


def run_block(
    shards_count, prefix_count, tokens, cotangent, segments, vec, prefix_low, weights
):
    length, width = tokens.shape
    heads = width // HEAD_DIM
    hbm = pl.BlockSpec(memory_space=pl.ANY)
    vmem = pl.BlockSpec(memory_space=pltpu.VMEM)
    return pl.pallas_call(
        functools.partial(block_kernel, shards_count, prefix_count),
        out_shape=(
            jax.ShapeDtypeStruct((length, width), bf16),
            jax.ShapeDtypeStruct((length, width), f32),
            jax.ShapeDtypeStruct((PAD, 2 * width), f32),
        ),
        in_specs=[hbm, hbm, vmem, vmem, vmem, vmem, hbm],
        out_specs=(hbm, hbm, vmem),
        scratch_shapes=[
            pltpu.VMEM(weights.shape, bf16),
            pltpu.VMEM((length, width), bf16),
            pltpu.VMEM((length, width), bf16),
            pltpu.VMEM((length, width), bf16),
            pltpu.VMEM((length, 3 * width), bf16),
            pltpu.VMEM((width, length), bf16),
            pltpu.VMEM((width, length), bf16),
            pltpu.VMEM((heads, length, length), bf16),
            pltpu.VMEM((length, length), f32),
            pltpu.VMEM((heads * PAD, width), bf16),
            pltpu.VMEM((heads * PAD, width), bf16),
            pltpu.VMEM((heads * PAD, length), f32),
            pltpu.VMEM((heads * PAD, length), bf16),
            pltpu.VMEM((heads * PAD, length), bf16),
            pltpu.VMEM((width, length), f32),
            pltpu.VMEM((length, width), f32),
            pltpu.VMEM((length, width), f32),
            pltpu.VMEM((length, width), f32),
            pltpu.VMEM((length, width), bf16),
            pltpu.VMEM((length, 3 * width), bf16),
            pltpu.SemaphoreType.DMA((4,)),
            pltpu.SemaphoreType.DMA((12,)),
        ],
        compiler_params=pltpu.CompilerParams(vmem_limit_bytes=66_000_000),
    )(
        tokens,
        cotangent,
        segments[:, None],
        segments[None, :],
        vec,
        prefix_low,
        weights,
    )


def shards(
    tokens,
    segment_ids,
    cotangent,
    norm_in_gain,
    norm_in_shift,
    qkv_weight,
    qkv_bias,
    proj_weight,
    proj_bias,
    norm_mid_gain,
    norm_mid_shift,
    up_weight,
    up_bias,
    down_weight,
    down_bias,
    prefix_table,
    first_weight,
    first_bias,
    second_weight,
    second_bias,
):
    width = tokens.shape[-1]
    unit = qkv_weight.shape[0]
    count = width // unit
    reps = lax.axis_size("rep")
    prefix_count = prefix_table.shape[0]
    local = jnp.concatenate(
        [qkv_weight[:, b * width : (b + 1) * width] for b in range(3)]
        + [proj_weight]
        + [up_weight[:, b * width : (b + 1) * width] for b in range(4)]
        + [down_weight],
        axis=0,
    )
    share = local.shape[0] // reps
    mine = lax.dynamic_slice_in_dim(local, lax.axis_index("rep") * share, share, axis=0)
    weights = lax.all_gather(mine, ("dp", "rep"), axis=0, tiled=True).reshape(
        count, local.shape[0], width
    )
    small = jnp.concatenate(
        [
            part.reshape(-1, unit)
            for part in (
                norm_in_gain,
                norm_in_shift,
                proj_bias,
                norm_mid_gain,
                norm_mid_shift,
                down_bias,
            )
        ]
        + [qkv_bias.reshape(3, unit), up_bias.reshape(4, unit)],
        axis=0,
    )
    spread = lax.all_gather(small, "dp", axis=0)

    def line(i):
        return spread[:, i].reshape(1, width)

    vec = jnp.concatenate(
        [
            line(0),
            line(1),
            spread[:, 6:9].reshape(3, width),
            line(2),
            line(3),
            line(4),
            spread[:, 9:13].reshape(4, width),
            line(5),
            jnp.zeros((3, width), bf16),
        ],
        axis=0,
    ).astype(f32)
    hidden = jnp.tanh(
        jnp.dot(prefix_table, first_weight, preferred_element_type=f32) + first_bias.astype(f32)
    )
    hidden_low = hidden.astype(bf16)
    part = jnp.dot(hidden_low, second_weight, preferred_element_type=f32)
    part = lax.psum(part, "rep") + second_bias.astype(f32)
    prefix_kv = lax.all_gather(part, "dp", axis=1, tiled=True)
    prefix_low = jnp.pad(prefix_kv.astype(bf16), ((0, PAD - prefix_count), (0, 0)))
    activations, input_grad, prefix_grad = run_block(
        count,
        prefix_count,
        tokens[0],
        cotangent[0],
        segment_ids[0],
        vec,
        prefix_low,
        weights,
    )
    prefix_grad = prefix_grad[:prefix_count]
    owned = lax.psum(
        lax.psum_scatter(prefix_grad, "dp", scatter_dimension=1, tiled=True), "rep"
    )
    hidden_values = hidden_low.astype(f32)
    second_weight_grad = jnp.dot(
        hidden_values.T, owned, precision=highest, preferred_element_type=f32
    )
    second_bias_grad = jnp.sum(owned, axis=0)
    hidden_part = jnp.dot(
        owned, second_weight.astype(f32).T, precision=highest, preferred_element_type=f32
    )
    grad_hidden = lax.psum(hidden_part, "dp")
    grad_inner = grad_hidden * (1.0 - hidden * hidden)
    first_weight_grad = jnp.dot(
        prefix_table.astype(f32).T, grad_inner, precision=highest, preferred_element_type=f32
    )
    first_bias_grad = jnp.sum(grad_inner, axis=0)
    table_part = jnp.dot(
        grad_inner, first_weight.astype(f32).T, precision=highest, preferred_element_type=f32
    )
    prefix_table_grad = lax.psum(table_part, "rep")
    return (
        activations[None],
        input_grad[None],
        prefix_table_grad,
        first_weight_grad,
        first_bias_grad,
        second_weight_grad,
        second_bias_grad,
        prefix_kv,
    )


def solution(mesh):
    in_specs = (
        P(("dp", "rep"), None, None),
        P(("dp", "rep"), None),
        P(("dp", "rep"), None, None),
        P("dp"),
        P("dp"),
        P("dp", None),
        P("dp"),
        P("dp", None),
        P("dp"),
        P("dp"),
        P("dp"),
        P("dp", None),
        P("dp"),
        P("dp", None),
        P("dp"),
        P(),
        P(None, "rep"),
        P("rep"),
        P("rep", "dp"),
        P("dp"),
    )
    out_specs = (
        P(("dp", "rep"), None, None),
        P(("dp", "rep"), None, None),
        P(),
        P(None, "rep"),
        P("rep"),
        P("rep", "dp"),
        P("dp"),
        P(),
    )
    return jax.shard_map(shards, mesh=mesh, in_specs=in_specs, out_specs=out_specs, check_vma=False)
```

```python
import functools

import jax
import jax.numpy as jnp
from jax import lax
from jax.experimental import pallas as pl
from jax.experimental.pallas import tpu as pltpu
from jax.sharding import PartitionSpec as P

HEAD_DIM = 64
PAIR = 2 * HEAD_DIM
CHUNK = 512
PAD = 16
ROWS = 128
SLOTS = 12
PARTS = 4
LEAD = 2
MESH = pl.DeviceIdType.MESH
VEC_ROWS = ((0, 1), (1, 1), (2, 3), (5, 1), (6, 1), (7, 1), (8, 4), (12, 1))

eps_norm = 1e-05
neg_fill = -1e30
highest = lax.Precision.HIGHEST
f32 = jnp.float32
bf16 = jnp.bfloat16

NN = (((1,), (0,)), ((), ()))
NT = (((1,), (1,)), ((), ()))
TN = (((0,), (0,)), ((), ()))


def mm(left, right, dims=NN):
    return lax.dot_general(left, right, dims, preferred_element_type=f32)


def normalise(values):
    centred = values - jnp.mean(values, axis=-1, keepdims=True)
    variance = jnp.mean(centred * centred, axis=-1, keepdims=True)
    inverse = lax.rsqrt(variance + eps_norm)
    return centred * inverse, inverse


def norm_backward(values, gain, upstream):
    unit, inverse = normalise(values)
    scaled = upstream * gain
    return inverse * (
        scaled
        - jnp.mean(scaled, axis=-1, keepdims=True)
        - unit * jnp.mean(scaled * unit, axis=-1, keepdims=True)
    )


def neighbours(dp, rep):
    return (dp + 1 - 2 * (dp % 2), rep), (dp, rep + 2 - 4 * (rep // 2)), (dp, rep + 1 - 2 * (rep % 2))


def remote(src, dst, send_sem, recv_sem, device):
    return pltpu.make_async_remote_copy(
        src_ref=src,
        dst_ref=dst,
        send_sem=send_sem,
        recv_sem=recv_sem,
        device_id=device,
        device_id_type=MESH,
    )


def pick(z, values):
    out = jnp.int32(values[-1])
    for i in range(len(values) - 2, -1, -1):
        out = jnp.where(z == i, values[i], out)
    return out


def gather_steps(weights, own_sem, sib_sem, z_sem, y_sem, x_sem, send_sem, zsend_sem):
    dp = lax.axis_index("dp")
    rep = lax.axis_index("rep")
    z = dp // 2
    x = dp % 2
    y = rep // 2
    core = rep % 2
    cols = weights.shape[2] // 2
    planes = [pick(z, v) for v in ((1, 0, 1, 2), (2, 2, 3, 1), (3, 3, 0, 0))]
    hops = [pick(z, v) for v in ((1, 1, 1, 1), (2, 1, 1, 2), (3, 2, 2, 3))]
    x_dev, y_dev, core_dev = neighbours(dp, rep)
    up = (dp + 2, rep)
    down = (dp - 2, rep)
    x_shard = dp + 1 - 2 * x

    def region(slot, shard, count, row, rows):
        return weights.at[
            pl.ds(shard, count),
            pl.ds(pl.multiple_of(slot * ROWS + row, 16), rows),
            pl.ds(pl.multiple_of(core * cols, 128), cols),
        ]

    def move(part, send, recv, device):
        return remote(part, part, send, recv, device)

    z_row = 16 * (4 * y + x)
    y_row = 16 * (4 * (1 - y) + x)
    x_row = 16 * (4 * y + 3 * x)
    far_row = 16 * (4 * (1 - y) + 3 * x)

    def guarded(slot, f):
        pl.when((slot >= 0) & (slot < SLOTS))(functools.partial(f, slot))

    def send_own(s):
        move(region(s, dp, 1, 0, ROWS), send_sem.at[s], own_sem.at[s], x_dev).start()

    def take_own(s):
        part = region(s, x_shard, 1, 0, ROWS)
        move(part, send_sem.at[s], own_sem.at[s], x_dev).wait_recv()
        plane = region(s, 2 * z, 2, z_row, 48)

        @pl.when(z < 3)
        def _():
            move(plane, zsend_sem.at[s, 0], z_sem.at[s, z], up).start()

        @pl.when(z > 0)
        def _():
            move(plane, zsend_sem.at[s, 1], z_sem.at[s, z], down).start()

        move(part, send_sem.at[s], sib_sem.at[s], core_dev).start()

    def take_z(i, s):
        p = planes[i]
        part = region(s, 2 * p, 2, z_row, 48)
        move(part, zsend_sem.at[s, 2 + i], z_sem.at[s, p], x_dev).wait_recv()

        @pl.when((p < z) & (z < 3))
        def _():
            move(part, zsend_sem.at[s, 2 + i], z_sem.at[s, p], up).start()

        @pl.when((p > z) & (z > 0))
        def _():
            move(part, zsend_sem.at[s, 2 + i], z_sem.at[s, p], down).start()

        move(part, send_sem.at[s], y_sem.at[s, p], y_dev).start()
        move(region(s, 2 * p, 2, x_row, 16), send_sem.at[s], x_sem.at[s, p], x_dev).start()

    def take_y(i, s):
        p = planes[i]
        move(region(s, 2 * p, 2, y_row, 48), send_sem.at[s], y_sem.at[s, p], y_dev).wait_recv()
        move(region(s, 2 * p, 2, far_row, 16), send_sem.at[s], x_sem.at[s, p], x_dev).start()

    def take_x(i, s):
        p = planes[i]
        move(region(s, 2 * p, 2, 0, 32), send_sem.at[s], x_sem.at[s, p], x_dev).wait_recv()
        move(region(s, 2 * p, 2, 0, ROWS), send_sem.at[s], sib_sem.at[s], core_dev).start()

    def take_core(s):
        move(region(s, 0, 7, 0, ROWS), send_sem.at[s], sib_sem.at[s], core_dev).wait_recv()

    def step(u):
        t = u // PARTS
        part = u % PARTS

        @pl.when(part == 0)
        def _():
            guarded(t, send_own)
            guarded(t - LEAD, take_own)
            guarded(t - LEAD - hops[0], functools.partial(take_z, 0))

        @pl.when(part == 1)
        def _():
            guarded(t - LEAD - hops[1], functools.partial(take_z, 1))
            guarded(t - LEAD - hops[2], functools.partial(take_z, 2))

        @pl.when(part == 2)
        def _():
            for i in range(3):
                guarded(t - LEAD - 1 - hops[i], functools.partial(take_y, i))

        @pl.when(part == 3)
        def _():
            for i in range(3):
                guarded(t - LEAD - 2 - hops[i], functools.partial(take_x, i))
            guarded(t - LEAD - 6, take_core)

    def finish():
        @pl.loop(0, SLOTS)
        def _(s):
            sent = weights.at[pl.ds(0, 4), pl.ds(0, 752), pl.ds(0, cols // 2)]
            move(sent, send_sem.at[s], own_sem.at[s], x_dev).wait_send()
            plane = region(s, 0, 2, 0, 48)

            def done(i):
                move(plane, zsend_sem.at[s, i], z_sem.at[s, z], x_dev).wait_send()

            pl.when(z < 3)(functools.partial(done, 0))
            pl.when(z > 0)(functools.partial(done, 1))
            for i in range(3):
                p = planes[i]
                pl.when(((p < z) & (z < 3)) | ((p > z) & (z > 0)))(functools.partial(done, 2 + i))

    return step, finish


def exchange(ref, own, sems, axis, count):
    dp = lax.axis_index("dp")
    rep = lax.axis_index("rep")

    def start(source=None):
        for i in range(1, count):
            if axis == "dp":
                device = (lax.rem(dp + i, count), rep)
                slot = lax.rem(dp + i, count)
            else:
                device = (dp, lax.rem(rep + i, count))
                slot = lax.rem(rep + i, count)
            src = ref.at[own] if source is None else source.at[slot]
            remote(src, ref.at[own], sems.at[0], sems.at[1], device).start()

    def wait():
        rest = ref.at[pl.ds(0, count - 1)]
        both = remote(rest, rest, sems.at[0], sems.at[1], (dp, lax.rem(rep + 1, 4)))
        both.wait_recv()
        both.wait_send()

    return start, wait


def block_kernel(comm, count, prefix_count, *refs):
    refs = list(refs)

    def take(number):
        out = refs[:number]
        del refs[:number]
        return out

    tokens_hbm, cotangent_hbm, seg_row = take(3)
    if comm:
        (small, table, first_w, first_b, second_w, second_b) = take(6)
        (qkv_hbm, proj_hbm, up_hbm, down_hbm) = take(4)
        (
            activations_hbm,
            input_grad_hbm,
            table_grad,
            first_w_grad,
            first_b_grad,
            second_w_grad,
            second_b_grad,
            prefix_kv,
        ) = take(8)
    else:
        small, prefix_in, weights_hbm = take(3)
        activations_hbm, input_grad_hbm, prefix_grad_out = take(3)
    (
        weights,
        tok,
        cot,
        normed,
        packed,
        keys_t,
        values_t,
        probs,
        bias_t,
        key_pre,
        value_pre,
        pre_f32,
        pre_probs,
        pre_dscore,
        mixed_t,
        acc_a,
        acc_g,
        resid,
        attended,
        grad_packed,
        vec_ref,
        sem,
        wsem,
    ) = take(23)
    if comm:
        (small_all, part_all, kv_all, grad_blocks, red_dp, red_rep, red_hidden, red_table) = take(8)
        (small_sem, part_sem, kv_sem, red_sem) = take(4)
        gather_sems = take(7)

    length, width = tok.shape
    heads = width // HEAD_DIM
    unit = width // count
    half = width // CHUNK
    scale = HEAD_DIM ** (-0.5)
    group = count // half
    zero = jnp.zeros((), bf16)

    copies = [
        pltpu.make_async_copy(tokens_hbm, tok, sem.at[0]),
        pltpu.make_async_copy(cotangent_hbm, cot, sem.at[1]),
    ]
    if comm:
        dp = lax.axis_index("dp")
        rep = lax.axis_index("rep")
        pieces = [qkv_hbm.at[:, b * width : (b + 1) * width] for b in range(3)] + [proj_hbm]
        pieces += [down_hbm]
        pieces += [up_hbm.at[:, b * width : (b + 1) * width] for b in range(4)]
        row = 0
        loads = []
        for i, piece in enumerate(pieces):
            rows = 4 * unit if i == 4 else unit
            loads.append(
                pltpu.make_async_copy(piece, weights.at[dp, pl.ds(row, rows), :], wsem.at[i])
            )
            row += rows
        for c in loads[:4] + copies + loads[4:]:
            c.start()
        barrier = pltpu.get_barrier_semaphore()
        for i in range(1, 8):
            pl.semaphore_signal(
                barrier, inc=1, device_id=(lax.rem(dp + i, 8), rep), device_id_type=MESH
            )
        for i in range(1, 4):
            pl.semaphore_signal(
                barrier, inc=1, device_id=(dp, lax.rem(rep + i, 4)), device_id_type=MESH
            )
        small_all[dp] = small[...]
        hidden = jnp.tanh(mm(table[...], first_w[...]) + first_b[...].astype(f32))
        hidden_low = hidden.astype(bf16)
        part_all[rep] = jnp.zeros(part_all.shape[1:], f32)
        part_all[rep, :prefix_count, :] = mm(hidden_low, second_w[...])
        for c in loads:
            c.wait()
        pl.semaphore_wait(barrier, 10)
        step, finish_gather = gather_steps(weights, *gather_sems)
        small_start, small_wait = exchange(small_all, dp, small_sem, "dp", 8)
        part_start, part_wait = exchange(part_all, rep, part_sem, "rep", 4)
        kv_start, kv_wait = exchange(kv_all, dp, kv_sem, "dp", 8)
        step(0)
        small_start()
        part_start()
        now = [1]

        def run(number):
            if number > 0:
                first = now[0]
                now[0] += number
                pl.loop(first, first + number)(step)

        def until(slot):
            run(PARTS * (slot + LEAD + 7) - now[0])

    else:
        loads = [
            pltpu.make_async_copy(
                weights_hbm.at[:, pl.ds(b * unit, unit), :],
                weights.at[:, pl.ds(b * unit, unit), :],
                wsem.at[b],
            )
            for b in range(12)
        ]
        for c in copies + loads:
            c.start()
        for c in loads:
            c.wait()

    def in_weight(block, col):
        return weights[:, pl.ds(block * unit, unit), pl.ds(col, CHUNK)].reshape(width, CHUNK)

    def out_weight(block, c):
        return weights[pl.ds(c * group, group), pl.ds(block * unit, unit), :].reshape(CHUNK, width)

    def vec(row, col=0, size=None):
        return vec_ref[pl.ds(row, 1), pl.ds(col, width if size is None else size)]

    rows_step = 128
    row_steps = length // rows_step

    seg_col = jnp.broadcast_to(seg_row[...].astype(f32), (rows_step, length)).T
    attended[...] = jnp.concatenate([seg_col] * (width // rows_step), axis=1).astype(bf16)

    @pl.loop(0, row_steps)
    def _(r):
        rows = pl.ds(r * rows_step, rows_step)
        key_pos = lax.broadcasted_iota(jnp.int32, (rows_step, length), 0) + r * rows_step
        query_pos = lax.broadcasted_iota(jnp.int32, (rows_step, length), 1)
        same = attended[rows, :length].astype(f32) == seg_row[...].astype(f32)
        bias_t[rows, :] = jnp.where(same & (key_pos <= query_pos), 0.0, neg_fill)

    if comm:
        run(3)
        small_wait()
        for j in range(count):
            part = small_all[j].astype(f32)
            row = 0
            for first, number in VEC_ROWS:
                for r in range(number):
                    at = (j * number + r) * unit
                    col = at % width
                    vec_ref[first + at // width : first + at // width + 1, col : col + unit] = part[
                        row : row + 1
                    ]
                    row += 1
    else:
        vec_ref[...] = small[...]

    copies[0].wait()
    if comm:
        first_norm = now[0]
        now[0] += row_steps

    @pl.loop(0, row_steps)
    def _(r):
        rows = pl.ds(r * rows_step, rows_step)
        unit_rows, _ = normalise(tok[rows, :].astype(f32))
        normed[rows, :] = (unit_rows * vec(0) + vec(1)).astype(bf16)
        if comm:
            step(first_norm + r)

    if comm:
        part_wait()
        total = part_all[0] + part_all[1] + part_all[2] + part_all[3]
        kv_all[dp] = total + second_b[...].astype(f32)
        run(4)
        kv_start()

    def project(s):
        block = s // half
        col = (s % half) * CHUNK
        out = mm(normed[...], in_weight(block, col)) + vec(2 + block, col, CHUNK)
        factor = jnp.where(block == 0, scale, 1.0).astype(bf16)
        packed[:, pl.ds(s * CHUNK, CHUNK)] = out.astype(bf16) * factor

    if comm:
        until(0)
        first_qkv = now[0]
        now[0] += 3 * PARTS

        @pl.loop(0, 3 * half)
        def _(s):
            project(s)
            for k in range(PARTS // half):
                step(first_qkv + s * (PARTS // half) + k)
    else:
        pl.loop(0, 3 * half)(project)

    head_of_row = lax.broadcasted_iota(jnp.int32, (heads * PAD, width), 0) // PAD
    head_of_col = lax.broadcasted_iota(jnp.int32, (heads * PAD, width), 1) // HEAD_DIM
    own_head = head_of_row == head_of_col
    if comm:
        kv_wait()
        whole_kv = jnp.concatenate([kv_all[j] for j in range(count)], axis=1)
        prefix_kv[...] = whole_kv[:prefix_count]
        prefix_low = whole_kv.astype(bf16)
    else:
        prefix_low = prefix_in[...]
    key_pre[...] = jnp.where(own_head, jnp.concatenate([prefix_low[:, :width]] * heads, axis=0), zero)
    value_pre[...] = jnp.where(
        own_head, jnp.concatenate([prefix_low[:, width:]] * heads, axis=0), zero
    )
    pre_scores = mm(key_pre[...], packed[:, :width], NT)
    pad_row = lax.broadcasted_iota(jnp.int32, pre_scores.shape, 0) % PAD
    pre_f32[...] = jnp.where(pad_row < prefix_count, pre_scores, neg_fill)

    q_blocks = ((0, length // 2, length // 2), (length // 2, length // 2, length))
    lane_head = lax.broadcasted_iota(jnp.int32, (length, PAIR), 1) // HEAD_DIM

    if comm:
        first_attend = now[0]
        now[0] += heads // 2

    @pl.loop(0, heads // 2)
    def _(p):
        col = pl.multiple_of(p * PAIR, PAIR)
        q_pair = packed[:, pl.ds(col, PAIR)]
        k_pair = packed[:, pl.ds(width + col, PAIR)]
        v_pair = packed[:, pl.ds(2 * width + col, PAIR)]
        keys_t[pl.ds(col, PAIR), :] = k_pair.T
        values_t[pl.ds(col, PAIR), :] = v_pair.T
        for e in range(2):
            k_head = jnp.where(lane_head == e, k_pair, zero)
            head = 2 * p + e
            feat = pl.ds(pl.multiple_of(head * HEAD_DIM, HEAD_DIM), HEAD_DIM)
            pre_rows = pl.ds(pl.multiple_of(head * PAD, PAD), PAD)
            for q0, q_size, k_size in q_blocks:
                s = mm(k_head[:k_size], q_pair[q0 : q0 + q_size], NT)
                s = s + bias_t[:k_size, q0 : q0 + q_size]
                sp = pre_f32[pre_rows, q0 : q0 + q_size]
                top = jnp.maximum(
                    jnp.max(s, axis=0, keepdims=True), jnp.max(sp, axis=0, keepdims=True)
                )
                s = jnp.exp(s - top)
                sp = jnp.exp(sp - top)
                inverse = 1.0 / (
                    jnp.sum(s, axis=0, keepdims=True) + jnp.sum(sp, axis=0, keepdims=True)
                )
                own = (s * inverse).astype(bf16)
                probs[head, :k_size, q0 : q0 + q_size] = own
                pre_probs[pre_rows, q0 : q0 + q_size] = (sp * inverse).astype(bf16)
                mixed_t[feat, q0 : q0 + q_size] = mm(values_t[feat, :k_size], own)
        if comm:
            step(first_attend + p)

    if comm:
        first_turn = now[0]
        now[0] += width // 128

    @pl.loop(0, width // 128)
    def _(i):
        rows = pl.ds(pl.multiple_of(i * 128, 128), 128)
        full = mixed_t[rows, :] + mm(value_pre[:, rows], pre_probs[...], TN)
        attended[:, rows] = full.T.astype(bf16)
        if comm:
            step(first_turn + i)

    @pl.loop(0, half)
    def _(c):
        cols = pl.ds(pl.multiple_of(c * CHUNK, CHUNK), CHUNK)
        out = mm(attended[...], in_weight(3, c * CHUNK)) + vec(5, c * CHUNK, CHUNK)
        resid[:, cols] = tok[:, cols].astype(f32) + out

    if comm:
        first_mid = now[0]
        now[0] += row_steps

    @pl.loop(0, row_steps)
    def _(r):
        rows = pl.ds(r * rows_step, rows_step)
        unit_rows, _ = normalise(resid[rows, :])
        normed[rows, :] = (unit_rows * vec(6) + vec(7)).astype(bf16)
        if comm:
            step(first_mid + r)

    copies[1].wait()

    ff_steps = 4 * half
    root = 0.7978845608028654
    cube = 0.044715

    def feed(i, mid_step=lambda k: None):
        col = (i % half) * CHUNK
        w_up = in_weight(8 + i // half, col)
        w_down = weights[
            pl.ds(i * (count // ff_steps), count // ff_steps), pl.ds(4 * unit, 4 * unit), :
        ].reshape(CHUNK, width)
        pre = mm(normed[...], w_up) + vec(8 + i // half, col, CHUNK)
        square = pre * pre
        t = jnp.tanh(root * (pre + cube * (square * pre)))
        act = (0.5 * pre * (1.0 + t)).astype(bf16)
        slope = 0.5 * (1.0 + t) + (0.5 * root) * pre * (1.0 - t * t) * (
            1.0 + (3.0 * cube) * square
        )
        grad_act = mm(cot[...], w_down, NT)
        grad_pre = (grad_act * slope).astype(bf16)
        mid_step(0)
        acc_a[...] = jnp.where(i == 0, 0.0, acc_a[...]) + mm(act, w_down)
        mid_step(1)
        acc_g[...] = jnp.where(i == 0, 0.0, acc_g[...]) + mm(grad_pre, w_up, NT)

    if comm:
        until(8)
        first_feed = now[0]
        now[0] += 3 * PARTS

        @pl.loop(0, 6)
        def _(i):
            feed(i, lambda k: step(first_feed + 2 * i + k))

        pl.loop(6, ff_steps)(feed)
    else:
        pl.loop(0, ff_steps)(feed)

    @pl.loop(0, row_steps)
    def _(r):
        rows = pl.ds(r * rows_step, rows_step)
        attended[rows, :] = (resid[rows, :] + acc_a[rows, :] + vec(12)).astype(bf16)
        grad = cot[rows, :].astype(f32) + norm_backward(resid[rows, :], vec(6), acc_g[rows, :])
        acc_g[rows, :] = grad
        normed[rows, :] = grad.astype(bf16)

    out_copy = pltpu.make_async_copy(attended, activations_hbm, sem.at[2])
    out_copy.start()
    for c in range(half):
        cot[:, c * CHUNK : (c + 1) * CHUNK] = mm(normed[...], out_weight(3, c), NT).astype(bf16)
    pre_f32[...] = mm(value_pre[...], cot[...], NT)

    @pl.loop(0, heads // 2)
    def _(p):
        col = pl.multiple_of(p * PAIR, PAIR)
        q_pair = packed[:, pl.ds(col, PAIR)]
        v_pair = packed[:, pl.ds(2 * width + col, PAIR)]
        g_pair = cot[:, pl.ds(col, PAIR)]
        key_grad = jnp.zeros((length, PAIR), f32)
        value_grad = jnp.zeros((length, PAIR), f32)
        for e in range(2):
            own_lanes = lane_head == e
            v_head = jnp.where(own_lanes, v_pair, zero)
            q_head = jnp.where(own_lanes, q_pair, zero)
            g_head = jnp.where(own_lanes, g_pair, zero)
            head = 2 * p + e
            feat = pl.ds(pl.multiple_of(head * HEAD_DIM, HEAD_DIM), HEAD_DIM)
            pre_rows = pl.ds(pl.multiple_of(head * PAD, PAD), PAD)
            for q0, q_size, k_size in q_blocks:
                dp_own = mm(v_head[:k_size], g_pair[q0 : q0 + q_size], NT)
                own_low = probs[head, :k_size, q0 : q0 + q_size]
                own = own_low.astype(f32)
                pre = pre_probs[pre_rows, q0 : q0 + q_size].astype(f32)
                pre_dp = pre_f32[pre_rows, q0 : q0 + q_size]
                dot = jnp.sum(own * dp_own, axis=0, keepdims=True) + jnp.sum(
                    pre * pre_dp, axis=0, keepdims=True
                )
                ds = (own * (dp_own - dot)).astype(bf16)
                pre_dscore[pre_rows, q0 : q0 + q_size] = (pre * (pre_dp - dot)).astype(bf16)
                mixed_t[feat, q0 : q0 + q_size] = mm(keys_t[feat, :k_size], ds)
                dk = mm(ds, q_head[q0 : q0 + q_size])
                dv = mm(own_low, g_head[q0 : q0 + q_size])
                if k_size < length:
                    fill = jnp.zeros((length - k_size, PAIR), f32)
                    dk = jnp.concatenate([dk, fill], axis=0)
                    dv = jnp.concatenate([dv, fill], axis=0)
                key_grad = key_grad + dk
                value_grad = value_grad + dv
        grad_packed[:, pl.ds(width + col, PAIR)] = key_grad.astype(bf16)
        grad_packed[:, pl.ds(2 * width + col, PAIR)] = value_grad.astype(bf16)

    sums = []
    for left, right in ((pre_dscore, packed), (pre_probs, cot)):
        whole = jnp.where(own_head, mm(left[...], right[:, :width]), 0.0)
        total = whole[:PAD]
        for h in range(1, heads):
            total = total + whole[h * PAD : (h + 1) * PAD]
        sums.append(total)
    prefix_grad = jnp.concatenate(sums, axis=1)
    if comm:
        wide = 2 * unit
        for j in range(count):
            grad_blocks[j] = prefix_grad[:, j * wide : (j + 1) * wide]
        red_dp[dp] = grad_blocks[dp]
    else:
        prefix_grad_out[...] = prefix_grad

    @pl.loop(0, width // 128)
    def _(i):
        rows = pl.ds(pl.multiple_of(i * 128, 128), 128)
        full = mixed_t[rows, :] + mm(key_pre[:, rows], pre_dscore[...], TN)
        grad_packed[:, rows] = (full * scale).T.astype(bf16)

    def back_project(c):
        total = None
        for b in range(3):
            term = mm(grad_packed[:, b * width : (b + 1) * width], out_weight(b, c), NT)
            total = term if total is None else total + term
        acc_a[:, c * CHUNK : (c + 1) * CHUNK] = total

    def back_norm(r):
        rows = pl.ds(r * rows_step, rows_step)
        acc_g[rows, :] += norm_backward(tok[rows, :].astype(f32), vec(0), acc_a[rows, :])

    if comm:
        dp_start, dp_wait = exchange(red_dp, dp, red_sem.at[0], "dp", 8)
        rep_start, rep_wait = exchange(red_rep, rep, red_sem.at[1], "rep", 4)
        hid_start, hid_wait = exchange(red_hidden, dp, red_sem.at[2], "dp", 8)
        tab_start, tab_wait = exchange(red_table, rep, red_sem.at[3], "rep", 4)

        def tree(ref, number):
            total = ref[0]
            for j in range(1, number):
                total = total + ref[j]
            return total

        def exact(left, right, dims):
            return lax.dot_general(
                left, right, dims, precision=highest, preferred_element_type=f32
            )

        dp_start(grad_blocks)
        back_project(0)
        dp_wait()
        red_rep[rep] = tree(red_dp, 8)
        rep_start()
        back_project(1)
        rep_wait()
        owned = tree(red_rep, 4)
        red_hidden[dp] = exact(owned, second_w[...].astype(f32), NT)
        pl.loop(0, 1)(back_norm)
        hid_start()
        owned_rows = owned[:prefix_count]
        hidden_again = jnp.tanh(mm(table[...], first_w[...]) + first_b[...].astype(f32))
        second_w_grad[...] = exact(hidden_again.astype(bf16).astype(f32), owned_rows, TN)
        second_b_grad[...] = jnp.sum(owned, axis=0, keepdims=True)
        pl.loop(1, 2)(back_norm)
        hid_wait()
        inner = tree(red_hidden, 8)[:prefix_count] * (1.0 - hidden_again * hidden_again)
        red_table[rep, :prefix_count, :] = exact(inner, first_w[...].astype(f32), NT)
        first_w_grad[...] = exact(table[...].astype(f32), inner, TN)
        first_b_grad[...] = jnp.sum(inner, axis=0, keepdims=True)
        tab_start()
        pl.loop(2, row_steps)(back_norm)
    else:
        for c in range(half):
            back_project(c)
        pl.loop(0, row_steps)(back_norm)

    in_copy = pltpu.make_async_copy(acc_g, input_grad_hbm, sem.at[3])
    in_copy.start()
    if comm:
        tab_wait()
        table_grad[...] = tree(red_table, 4)[:prefix_count]
        finish_gather()
    out_copy.wait()
    in_copy.wait()


def run_block(comm, count, prefix_count, operands, weights_shape):
    length, width = operands[0].shape
    heads = width // HEAD_DIM
    hbm = pl.BlockSpec(memory_space=pl.ANY)
    vmem = pl.BlockSpec(memory_space=pltpu.VMEM)
    shape = jax.ShapeDtypeStruct
    scratch = [
        pltpu.VMEM(weights_shape, bf16),
        pltpu.VMEM((length, width), bf16),
        pltpu.VMEM((length, width), bf16),
        pltpu.VMEM((length, width), bf16),
        pltpu.VMEM((length, 3 * width), bf16),
        pltpu.VMEM((width, length), bf16),
        pltpu.VMEM((width, length), bf16),
        pltpu.VMEM((heads, length, length), bf16),
        pltpu.VMEM((length, length), f32),
        pltpu.VMEM((heads * PAD, width), bf16),
        pltpu.VMEM((heads * PAD, width), bf16),
        pltpu.VMEM((heads * PAD, length), f32),
        pltpu.VMEM((heads * PAD, length), bf16),
        pltpu.VMEM((heads * PAD, length), bf16),
        pltpu.VMEM((width, length), f32),
        pltpu.VMEM((length, width), f32),
        pltpu.VMEM((length, width), f32),
        pltpu.VMEM((length, width), f32),
        pltpu.VMEM((length, width), bf16),
        pltpu.VMEM((length, 3 * width), bf16),
        pltpu.VMEM((PAD, width), f32),
        pltpu.SemaphoreType.DMA((4,)),
        pltpu.SemaphoreType.DMA((12,)),
    ]
    outs = [shape((length, width), bf16), shape((length, width), f32)]
    out_specs = [hbm, hbm]
    if comm:
        hidden_units = operands[5].shape[1]
        kv_unit = operands[7].shape[1]
        in_specs = [hbm, hbm] + [vmem] * 7 + [hbm] * 4
        outs += [
            shape((prefix_count, width), f32),
            shape((width, hidden_units), f32),
            shape((1, hidden_units), f32),
            shape((hidden_units, kv_unit), f32),
            shape((1, kv_unit), f32),
            shape((prefix_count, kv_unit * count), f32),
        ]
        out_specs += [vmem] * 6
        scratch += [
            pltpu.VMEM((count, PAD, width // count), bf16),
            pltpu.VMEM((4, PAD, kv_unit), f32),
            pltpu.VMEM((count, PAD, kv_unit), f32),
            pltpu.VMEM((count, PAD, kv_unit), f32),
            pltpu.VMEM((count, PAD, kv_unit), f32),
            pltpu.VMEM((4, PAD, kv_unit), f32),
            pltpu.VMEM((count, PAD, hidden_units), f32),
            pltpu.VMEM((4, PAD, width), f32),
            pltpu.SemaphoreType.DMA((2,)),
            pltpu.SemaphoreType.DMA((2,)),
            pltpu.SemaphoreType.DMA((2,)),
            pltpu.SemaphoreType.DMA((4, 2)),
            pltpu.SemaphoreType.DMA((SLOTS,)),
            pltpu.SemaphoreType.DMA((SLOTS,)),
            pltpu.SemaphoreType.DMA((SLOTS, 4)),
            pltpu.SemaphoreType.DMA((SLOTS, 4)),
            pltpu.SemaphoreType.DMA((SLOTS, 4)),
            pltpu.SemaphoreType.DMA((SLOTS,)),
            pltpu.SemaphoreType.DMA((SLOTS, 5)),
        ]
        params = pltpu.CompilerParams(
            collective_id=0, has_side_effects=True, vmem_limit_bytes=66_500_000
        )
    else:
        in_specs = [hbm, hbm] + [vmem] * 3 + [hbm]
        outs += [shape((PAD, 2 * width), f32)]
        out_specs += [vmem]
        params = pltpu.CompilerParams(vmem_limit_bytes=66_500_000)
    return pl.pallas_call(
        functools.partial(block_kernel, comm, count, prefix_count),
        out_shape=tuple(outs),
        in_specs=in_specs,
        out_specs=tuple(out_specs),
        scratch_shapes=scratch,
        compiler_params=params,
    )(*operands)


def shards(
    tokens,
    segment_ids,
    cotangent,
    norm_in_gain,
    norm_in_shift,
    qkv_weight,
    qkv_bias,
    proj_weight,
    proj_bias,
    norm_mid_gain,
    norm_mid_shift,
    up_weight,
    up_bias,
    down_weight,
    down_bias,
    prefix_table,
    first_weight,
    first_bias,
    second_weight,
    second_bias,
):
    width = tokens.shape[-1]
    unit = qkv_weight.shape[0]
    count = width // unit
    reps = lax.axis_size("rep")
    prefix_count = prefix_table.shape[0]
    comm = count == 8 and reps == 4
    small = jnp.concatenate(
        [
            norm_in_gain,
            norm_in_shift,
            qkv_bias,
            proj_bias,
            norm_mid_gain,
            norm_mid_shift,
            up_bias,
            down_bias,
            jnp.zeros((3 * unit,), bf16),
        ]
    )
    if comm:
        operands = (
            tokens[0],
            cotangent[0],
            segment_ids,
            small.reshape(PAD, unit),
            prefix_table,
            first_weight,
            first_bias[None],
            second_weight,
            second_bias[None],
            qkv_weight,
            proj_weight,
            up_weight,
            down_weight,
        )
        (
            activations,
            input_grad,
            prefix_table_grad,
            first_weight_grad,
            first_bias_grad,
            second_weight_grad,
            second_bias_grad,
            prefix_kv,
        ) = run_block(True, count, prefix_count, operands, (count, 12 * unit, width))
        return (
            activations[None],
            input_grad[None],
            prefix_table_grad,
            first_weight_grad,
            first_bias_grad[0],
            second_weight_grad,
            second_bias_grad[0],
            prefix_kv,
        )
    local = jnp.concatenate(
        [qkv_weight[:, b * width : (b + 1) * width] for b in range(3)]
        + [proj_weight, down_weight]
        + [up_weight[:, b * width : (b + 1) * width] for b in range(4)],
        axis=0,
    )
    share = local.shape[0] // reps
    mine = lax.dynamic_slice_in_dim(local, lax.axis_index("rep") * share, share, axis=0)
    weights = lax.all_gather(mine, ("dp", "rep"), axis=0, tiled=True).reshape(
        count, local.shape[0], width
    )
    spread = lax.all_gather(small, "dp", axis=0)
    rows = []
    first = 0
    for number in (1, 1, 3, 1, 1, 1, 4, 1, 3):
        rows.append(spread[:, first : first + number * unit].reshape(number, width))
        first += number * unit
    vec = jnp.concatenate(rows, axis=0).astype(f32)
    hidden = jnp.tanh(
        jnp.dot(prefix_table, first_weight, preferred_element_type=f32) + first_bias.astype(f32)
    )
    hidden_low = hidden.astype(bf16)
    part = jnp.dot(hidden_low, second_weight, preferred_element_type=f32)
    part = lax.psum(part, "rep") + second_bias.astype(f32)
    prefix_kv = lax.all_gather(part, "dp", axis=1, tiled=True)
    prefix_low = jnp.pad(prefix_kv.astype(bf16), ((0, PAD - prefix_count), (0, 0)))
    activations, input_grad, prefix_grad = run_block(
        False,
        count,
        prefix_count,
        (tokens[0], cotangent[0], segment_ids, vec, prefix_low, weights),
        weights.shape,
    )
    prefix_grad = prefix_grad[:prefix_count]
    owned = lax.psum(
        lax.psum_scatter(prefix_grad, "dp", scatter_dimension=1, tiled=True), "rep"
    )
    hidden_values = hidden_low.astype(f32)
    second_weight_grad = jnp.dot(
        hidden_values.T, owned, precision=highest, preferred_element_type=f32
    )
    second_bias_grad = jnp.sum(owned, axis=0)
    hidden_part = jnp.dot(
        owned, second_weight.astype(f32).T, precision=highest, preferred_element_type=f32
    )
    grad_hidden = lax.psum(hidden_part, "dp")
    grad_inner = grad_hidden * (1.0 - hidden * hidden)
    first_weight_grad = jnp.dot(
        prefix_table.astype(f32).T, grad_inner, precision=highest, preferred_element_type=f32
    )
    first_bias_grad = jnp.sum(grad_inner, axis=0)
    table_part = jnp.dot(
        grad_inner, first_weight.astype(f32).T, precision=highest, preferred_element_type=f32
    )
    prefix_table_grad = lax.psum(table_part, "rep")
    return (
        activations[None],
        input_grad[None],
        prefix_table_grad,
        first_weight_grad,
        first_bias_grad,
        second_weight_grad,
        second_bias_grad,
        prefix_kv,
    )


def solution(mesh):
    in_specs = (
        P(("dp", "rep"), None, None),
        P(("dp", "rep"), None),
        P(("dp", "rep"), None, None),
        P("dp"),
        P("dp"),
        P("dp", None),
        P("dp"),
        P("dp", None),
        P("dp"),
        P("dp"),
        P("dp"),
        P("dp", None),
        P("dp"),
        P("dp", None),
        P("dp"),
        P(),
        P(None, "rep"),
        P("rep"),
        P("rep", "dp"),
        P("dp"),
    )
    out_specs = (
        P(("dp", "rep"), None, None),
        P(("dp", "rep"), None, None),
        P(),
        P(None, "rep"),
        P("rep"),
        P("rep", "dp"),
        P("dp"),
        P(),
    )
    return jax.shard_map(shards, mesh=mesh, in_specs=in_specs, out_specs=out_specs, check_vma=False)
```
